32 devices in a mesh: region: 4 (over y, x), cluster: 8 (over z, core).
Axes of the slice: x: 2, y: 2, z: 4, core: 2. Of those that a mesh axis runs over, the one named last changes fastest.
Arguments:
- pilots: bfloat16 [128, 1024, 1024], P(('region', 'cluster')), may hold values from -0.1875 to 0.1875
- estimate: bfloat16 [128, 8, 1024], P(('region', 'cluster')), may hold values from -6 to 6
- visible: int32 [128, 1024], P(('region', 'cluster')), may hold values from 0 to 65535, as said below
- blocks: int32 [128], P(('region', 'cluster')), may hold values from 4 to 8
- received: float32 [128, 8, 1024], P(('region', 'cluster')), may hold values from -6 to 6
- previous: float32 [128, 8, 1024], P(('region', 'cluster')), may hold values from -6 to 6
- onsager: float32 [128], P(('region', 'cluster')), may hold values from 0.2 to 0.8
- user_cluster: int32 [65536], replicated, may hold values from 0 to 15
- cluster_prior: float32 [16], replicated, may hold values from -4 to 0
Outputs:
- new_estimate: bfloat16 [128, 8, 1024], P(('region', 'cluster'))
- residual: float32 [128, 8, 1024], P(('region', 'cluster'))
- posterior: float32 [65536], P(('region', 'cluster'))
The draws below stay inside these ranges and needn't reach their ends.
Inputs may be any that keep to these rules, and one draw needn't show every extreme that they name: Every draw has some access point with 8 live blocks. `visible`: users are numbered region by region, 2048 * 8 to a region, in the order of the devices along region+cluster. An access point hears only users of its own region or of the two regions beside it along region (the first and the last region are beside each other); most of the users it hears are of its own region.
All inputs are finite; a program needn't handle non-finite values.
Results may differ from the reference program's by a relative error of at most 0.0056.
Values sent between devices are 32-bit elements; how exact they have to be, the bound alone decides.
A program may use at most 192 MiB of HBM per device.

```python
import jax
import jax.numpy as jnp
from jax import lax

M = 8
L = 1024
ROW_BLOCK = 128
NB = 8
AP_DEV = 4
USER_CLUSTERS = 16
ROWS_AP = 1024
APS = 128
USERS = 65536
N_REGION = 4
N_CLUSTER = 8


def draw_visible(key, part):
    first, second = jax.random.split(jax.random.fold_in(key, 17))
    region_users = USERS // N_REGION
    home = jnp.arange(APS, dtype=jnp.int32) // AP_DEV // N_CLUSTER
    pick = jax.random.randint(first, (APS, ROWS_AP), 0, 20, dtype=jnp.int32)
    offset = jnp.where(pick == 0, -1, jnp.where(pick == 1, 1, 0)).astype(jnp.int32)
    region = (home[:, None] + offset + N_REGION) % N_REGION
    inside = jax.random.randint(second, (APS, ROWS_AP), 0, region_users, dtype=jnp.int32)
    return (region * region_users + inside).astype(jnp.int32)


def plant(drawn, key, least, top_value):
    spot = [jax.random.randint(jax.random.fold_in(key, axis), (), 0, length) for axis, length in enumerate(drawn.shape)]
    longest = drawn.shape.index(max(drawn.shape))
    neighbour = spot[:longest] + [(spot[longest] + 1) % drawn.shape[longest]] + spot[longest + 1:]
    return drawn.at[tuple(spot)].set(least).at[tuple(neighbour)].set(top_value)


def level_of(key, dims, shards, smallest, largest):
    factor_of = 1.0
    for dim, blocks in shards:
        heights = jax.random.uniform(jax.random.fold_in(jax.random.fold_in(key, 6), dim), (blocks,), jnp.float32, smallest / len(shards), largest / len(shards))
        factor_of = factor_of * jnp.repeat(jnp.exp(heights), dims[dim] // blocks).reshape((-1,) + (1,) * (len(dims) - 1 - dim))
    return factor_of


def bell_draw(key, dims, scale, bound, cuts=(), kind=jnp.bfloat16):
    level = level_of(key, dims, cuts, -0.22, 0.18) if cuts else 1.0
    values = jax.random.normal(key, dims, jnp.float32) * scale * level
    return jnp.minimum(jnp.maximum(values, -bound), bound).astype(kind)


def setup_inputs(seed: int = 0) -> dict:
    keys = jax.random.split(jax.random.key(seed), 10)
    pilots = bell_draw(keys[0], (APS, ROWS_AP, L), L ** -0.5, 0.1875, ((0, 32),))
    estimate = bell_draw(keys[1], (APS, M, ROWS_AP), 0.7, 6.0, ((0, 32),))
    visible = draw_visible(jax.random.fold_in(keys[9], 71), 0)
    blocks = plant(jax.random.randint(keys[3], (APS,), NB // 2, NB + 1), jax.random.fold_in(keys[3], 1), NB // 2, NB).astype(jnp.int32)
    received = bell_draw(keys[4], (APS, M, L), 1.0, 6.0, ((0, 32),), jnp.float32)
    previous = bell_draw(keys[5], (APS, M, L), 1.0, 6.0, ((0, 32),), jnp.float32)
    onsager = jnp.clip(0.2 + 0.6 * jax.random.uniform(keys[6], (APS,), jnp.float32) ** level_of(keys[6], (APS,), ((0, 32),), -0.2, 0.2), 0.2, 0.8)
    user_cluster = plant(jax.random.randint(keys[7], (USERS,), 0, USER_CLUSTERS), jax.random.fold_in(keys[7], 1), 0, USER_CLUSTERS - 1).astype(jnp.int32)
    cluster_prior = jnp.clip(jax.random.uniform(keys[8], (USER_CLUSTERS,), jnp.float32, -4.0, 0.0), -4.0, 0.0)
    return {"pilots": pilots, "estimate": estimate, "visible": visible, "blocks": blocks, "received": received, "previous": previous, "onsager": onsager, "user_cluster": user_cluster, "cluster_prior": cluster_prior}


epsilon = 1e-6


def reference(pilots, estimate, visible, blocks, received, previous, onsager, user_cluster, cluster_prior):
    live = (jnp.arange(ROWS_AP)[None, :] // ROW_BLOCK) < blocks[:, None]
    masked = jnp.where(live[:, None, :], estimate, jnp.zeros_like(estimate))

    def per_point(items):
        pil, est, sig, prev, coef = items
        product = jnp.dot(est, pil, preferred_element_type=jnp.float32)
        resid = sig - product + coef * prev
        spread = jnp.mean(resid * resid) + epsilon
        narrow = resid.astype(jnp.bfloat16)
        stat = est.astype(jnp.float32) + jnp.dot(narrow, pil.T, preferred_element_type=jnp.float32)
        return resid, stat, spread

    resid, stat, spread = lax.map(per_point, (pilots, masked, received, previous, onsager))
    energy = jnp.sum(stat * stat, axis=1)
    base = 0.5 * M * jnp.log(spread / (1.0 + spread))
    llr = base[:, None] + energy / (2.0 * spread * (1.0 + spread))[:, None]
    llr = jnp.where(live, llr, jnp.float32(0.0))
    combined = jax.ops.segment_sum(llr.reshape(-1), visible.reshape(-1), num_segments=USERS)
    posterior = jax.nn.sigmoid(combined + cluster_prior[user_cluster])
    rate = posterior[visible]
    fresh = rate[:, None, :] * stat / (1.0 + spread)[:, None, None]
    new_estimate = jnp.where(live[:, None, :], fresh, jnp.float32(0.0)).astype(jnp.bfloat16)
    return new_estimate, resid, posterior
```

```python
import jax
import jax.numpy as jnp
from jax import lax
from jax.experimental import pallas as pl
from jax.experimental.pallas import tpu as pltpu
from jax.sharding import PartitionSpec as P

ROW_BLOCK = 128
LANES = 128
TILE = 192
VMEM_LIMIT = 48 * 1024 * 1024
MESH = pl.DeviceIdType.MESH

epsilon = 1e-06


def window_places(visible, users, rows):
    regions, clusters = lax.axis_size("region"), lax.axis_size("cluster")
    lowest = lax.rem(lax.axis_index("region") + (regions - 1), regions) * (users // regions)
    shifted = visible - lowest
    shifted = jnp.where(shifted < 0, shifted + users, shifted)
    line = lax.div(shifted, LANES)
    device = lax.div(line, rows)
    place = lax.rem(device, 2) * (3 * clusters // 2) + lax.div(device, 2)
    return place * rows + lax.rem(line, rows), lax.rem(shifted, LANES)


def one_hot(row, count, start=0):
    place = lax.broadcasted_iota(jnp.int32, (count, row.shape[1]), 0).astype(jnp.float32)
    row = jnp.clip(row - start, -1, count).astype(jnp.float32)
    match = place.astype(jnp.bfloat16) == jnp.broadcast_to(row, place.shape).astype(jnp.bfloat16)
    return jnp.where(match, jnp.bfloat16(1), jnp.bfloat16(0))


def spread_rows(row, mask):
    count, width = mask.shape
    wide = jnp.broadcast_to(row, (16, width)).astype(jnp.bfloat16)
    return (mask.reshape(count // 16, 16, width) * wide[None]).reshape(count, width)


def flip(place, turn, count):
    result, weight = 0, 1
    while weight < count:
        digits = lax.div(place, weight) + lax.div(turn, weight)
        result = result + weight * lax.rem(digits, 2)
        weight *= 2
    return result


def main_kernel(
    pilots_hbm, estimate_hbm, visible_hbm, blocks_hbm, received_hbm, previous_hbm, onsager_hbm,
    labels_hbm, prior_hbm,
    fresh_out, resid_out, owned_out,
    pilots, estimate, visible, blocks, received, previous, onsager, labels, prior,
    alive, row_of, lane_of,
    scaled, nearby, selector, lanes, window, swapped, half, arrived, owned,
    load_sem, pilot_sem, swap_sem, sum_send, sum_recv, post_send, post_recv, relay_send, relay_recv,
):
    regions, clusters = lax.axis_size("region"), lax.axis_size("cluster")
    region, cluster = lax.axis_index("region"), lax.axis_index("cluster")
    core, chip, chips = lax.rem(cluster, 2), lax.div(cluster, 2), clusters // 2
    points, antennas, slots = estimate.shape
    rows = owned.shape[0]
    users = labels_hbm.shape[0] * LANES
    peers = 3 * chips
    half_rows = peers * rows
    odd = lax.rem(region, 2)
    served = region + 1 - 2 * odd
    home = (2 - 2 * odd) * chips + chip
    partner = (region, cluster + 1 - 2 * core)

    def part(ref, slot):
        return ref.at[pl.ds(pl.multiple_of(slot * rows, rows), rows), :]

    def side(which):
        return pl.ds(pl.multiple_of(which * half_rows, half_rows), half_rows)

    own_rows = pl.ds(pl.multiple_of((served * clusters + cluster) * rows, rows), rows)
    loads = [
        pltpu.make_async_copy(source, target, load_sem.at[i])
        for i, (source, target) in enumerate(
            [
                (visible_hbm, visible), (blocks_hbm, blocks), (estimate_hbm, estimate),
                (onsager_hbm, onsager), (received_hbm, received), (previous_hbm, previous),
                (prior_hbm, prior), (labels_hbm.at[own_rows, :], labels),
            ]
        )
    ]
    for copy in loads:
        copy.start()

    def fetch(i):
        return pltpu.make_async_copy(pilots_hbm.at[i], pilots.at[i], pilot_sem.at[i])

    @pl.loop(0, points)
    def _(i):
        fetch(i).start()

    def peer(j):
        place = flip(chip, chips - 1 - lax.div(j, 3), chips)
        which = lax.rem(j, 3)
        there = jnp.where(
            which == 0, served, jnp.where(which == 1, lax.rem(region + 2, regions), region)
        )
        step = jnp.where(which == 0, 1, jnp.where(which == 1, 2 * odd, 2 - 2 * odd))
        return step * chips + place, step * chips + chip, (there, place * 2 + core)

    barrier = pltpu.get_barrier_semaphore()
    pl.semaphore_signal(barrier, inc=1, device_id=partner, device_id_type=MESH)

    @pl.loop(0, peers - 1)
    def _(j):
        _, _, device = peer(j)
        pl.semaphore_signal(barrier, inc=1, device_id=device, device_id_type=MESH)

    window[...] = jnp.zeros(window.shape, jnp.float32)
    loads[0].wait()
    row_of[...], lane_of[...] = window_places(visible[...], users, rows)

    @pl.loop(0, points)
    def _(point):
        row = row_of[pl.ds(point, 1), :]
        lanes[point] = one_hot(lane_of[pl.ds(point, 1), :], LANES)

        @pl.loop(0, 2 * half_rows // TILE)
        def _(tile):
            start = pl.multiple_of(tile * TILE, TILE)
            selector[point, pl.ds(start, TILE), :] = one_hot(row, TILE, start)

    for copy in loads[1:]:
        copy.wait()
    slot_block = lax.broadcasted_iota(jnp.int32, (1, slots), 1) // ROW_BLOCK
    for point in range(points):
        live = jnp.where(slot_block < blocks[0:1, point : point + 1], 1.0, 0.0)
        alive[point : point + 1, :] = live
        estimate[point] = (estimate[point].astype(jnp.float32) * live).astype(jnp.bfloat16)
        received[point] += onsager[0:1, point : point + 1] * previous[point]

    def first(point):
        product = jnp.dot(estimate[point], pilots[point], preferred_element_type=jnp.float32)
        resid = received[point] - product
        resid_out[point] = resid
        square = jnp.sum(jnp.sum(resid * resid, axis=0, keepdims=True), axis=1, keepdims=True)
        spread = square / (antennas * resid.shape[1]) + epsilon
        base = 0.5 * antennas * jnp.log(spread / (1.0 + spread))
        factor = 1.0 / (2.0 * spread * (1.0 + spread))
        return resid.astype(jnp.bfloat16), base, factor, 1.0 / (1.0 + spread)

    def second(point, narrow):
        return lax.dot_general(
            narrow, pilots[point], (((1,), (1,)), ((), ())), preferred_element_type=jnp.float32
        )

    def weigh(point, projected, base, factor, shrink):
        live = alive[pl.ds(point, 1), :]
        stat = estimate[point].astype(jnp.float32) + projected
        energy = jnp.sum(stat * stat, axis=0, keepdims=True)
        llr = jnp.where(live > 0.5, base + energy * factor, 0.0)
        scaled[point] = jnp.where(live > 0.5, stat * shrink, 0.0)
        high = llr.astype(jnp.bfloat16).astype(jnp.float32)
        mask = lanes[point]
        return jnp.concatenate([spread_rows(high, mask), spread_rows(llr - high, mask)], axis=0)

    def gathered(point, values):
        both = lax.dot_general(
            selector[point], values, (((1,), (1,)), ((), ())), preferred_element_type=jnp.float32
        )
        return both[:, :LANES] + both[:, LANES:]

    fetch(0).wait()

    def turn(point, opened):
        narrow, *scales = opened
        later = jnp.minimum(point + 1, points - 1)

        @pl.when(point < points - 1)
        def _():
            fetch(point + 1).wait()

        projected = second(point, narrow)
        opened = first(later)
        window[...] += gathered(point, weigh(point, projected, *scales))
        return opened

    lax.fori_loop(0, points, turn, first(0))
    other, mine = side(1 - core), side(core)

    pl.semaphore_wait(barrier, peers)

    swap = pltpu.make_async_remote_copy(
        src_ref=window.at[other, :], dst_ref=swapped, send_sem=swap_sem.at[0],
        recv_sem=swap_sem.at[1], device_id=partner, device_id_type=MESH,
    )
    swap.start()
    total = jnp.zeros(owned.shape, jnp.float32)
    for k in range(prior.shape[1]):
        total = total + jnp.where(labels[...] == k, prior[0:1, k : k + 1], 0.0)
    swap.wait_recv()
    half[...] = window[mine, :] + swapped[...]

    def sum_copy(source, target, device):
        return pltpu.make_async_remote_copy(
            src_ref=part(half, source), dst_ref=part(arrived, target),
            send_sem=sum_send.at[source], recv_sem=sum_recv.at[target],
            device_id=device, device_id_type=MESH,
        )

    def post_copy(source, target, device):
        return pltpu.make_async_remote_copy(
            src_ref=owned, dst_ref=part(nearby, core * peers + target),
            send_sem=post_send.at[source], recv_sem=post_recv.at[target],
            device_id=device, device_id_type=MESH,
        )

    def relay_copy(place, slot):
        return pltpu.make_async_remote_copy(
            src_ref=part(nearby, place), dst_ref=part(nearby, place),
            send_sem=relay_send.at[slot], recv_sem=relay_recv.at[slot],
            device_id=partner, device_id_type=MESH,
        )

    @pl.loop(0, peers - 1)
    def _(j):
        slot, back, device = peer(j)
        sum_copy(slot, back, device).start()

    def collect(j, total):
        slot, _, device = peer(peers - 2 - j)
        sum_copy(slot, slot, device).wait_recv()
        return total + part(arrived, slot)[...]

    total = lax.fori_loop(0, peers - 1, collect, total + part(half, home)[...])
    posterior = jax.nn.sigmoid(total)
    owned[...] = posterior

    @pl.loop(0, peers - 1)
    def _(j):
        slot, back, device = peer(j)
        post_copy(slot, back, device).start()

    part(nearby, core * peers + home)[...] = posterior
    relay_copy(core * peers + home, home).start()

    @pl.loop(0, peers - 1)
    def _(j):
        slot, _, device = peer(peers - 2 - j)
        post_copy(slot, slot, device).wait_recv()
        relay_copy(core * peers + slot, slot).start()

    owned_out[...] = part(nearby, core * peers + chips + chip)[...]

    @pl.loop(0, peers - 1)
    def _(j):
        slot, back, device = peer(j)
        sum_copy(slot, back, device).wait_send()
        post_copy(slot, back, device).wait_send()

    swap.wait_send()

    @pl.loop(0, peers)
    def _(slot):
        relay_copy((1 - core) * peers + slot, slot).wait_recv()

    table = nearby[...].astype(jnp.bfloat16)

    @pl.loop(0, points)
    def _(point):
        picked = lax.dot_general(
            table, selector[point], (((0,), (0,)), ((), ())), preferred_element_type=jnp.float32
        )
        rate = jnp.sum(
            (picked.astype(jnp.bfloat16) * lanes[point]).astype(jnp.float32), axis=0, keepdims=True
        )
        fresh_out[point] = (rate * scaled[point]).astype(jnp.bfloat16)

    @pl.loop(0, peers)
    def _(slot):
        relay_copy(core * peers + slot, slot).wait_send()


def store_kernel(fresh, resid, owned, fresh_hbm, resid_hbm, owned_hbm, sem):
    copies = [
        pltpu.make_async_copy(resid, resid_hbm, sem.at[0]),
        pltpu.make_async_copy(fresh, fresh_hbm, sem.at[1]),
        pltpu.make_async_copy(owned, owned_hbm, sem.at[2]),
    ]
    for copy in copies:
        copy.start()
    for copy in copies:
        copy.wait()


def local(
    pilots, estimate, visible, blocks, received, previous, onsager, user_cluster, cluster_prior
):
    points, antennas, slots = estimate.shape
    length = pilots.shape[2]
    users = user_cluster.shape[0]
    regions, clusters = lax.axis_size("region"), lax.axis_size("cluster")
    rows = users // (regions * clusters) // LANES
    peers = 3 * clusters // 2
    half_rows = peers * rows
    f32, i32, bf16 = jnp.float32, jnp.int32, jnp.bfloat16
    kept = pl.BlockSpec(memory_space=pltpu.HBM)
    near = pl.BlockSpec(memory_space=pltpu.VMEM)
    vmem, dma = pltpu.VMEM, pltpu.SemaphoreType.DMA
    results = [
        ((points, antennas, slots), bf16),
        ((points, antennas, length), f32),
        ((rows, LANES), f32),
    ]
    made = pl.pallas_call(
        main_kernel,
        in_specs=[kept] * 9,
        out_specs=[near] * 3,
        out_shape=[pltpu.VMEM(*result) for result in results],
        scratch_shapes=[
            vmem((points, slots, length), bf16),
            vmem((points, antennas, slots), bf16),
            vmem((points, slots), i32),
            vmem((1, points), i32),
            vmem((points, antennas, length), f32),
            vmem((points, antennas, length), f32),
            vmem((1, points), f32),
            vmem((rows, LANES), i32),
            vmem((1, cluster_prior.shape[0]), f32),
            vmem((points, slots), f32),
            vmem((points, slots), i32),
            vmem((points, slots), i32),
            vmem((points, antennas, slots), f32),
            vmem((2 * half_rows, LANES), f32),
            vmem((points, 2 * half_rows, slots), bf16),
            vmem((points, LANES, slots), bf16),
            vmem((2 * half_rows, LANES), f32),
            vmem((half_rows, LANES), f32),
            vmem((half_rows, LANES), f32),
            vmem((half_rows, LANES), f32),
            vmem((rows, LANES), f32),
            dma((8,)), dma((points,)), dma((2,)),
            *[dma((peers,))] * 6,
        ],
        compiler_params=pltpu.CompilerParams(
            collective_id=0, has_side_effects=True, vmem_limit_bytes=VMEM_LIMIT
        ),
    )(
        *[
            pltpu.with_memory_space_constraint(operand, pltpu.HBM)
            for operand in (
                pilots, estimate, visible, blocks.reshape(1, -1), received, previous,
                onsager.reshape(1, -1), user_cluster.reshape(-1, LANES),
                cluster_prior.reshape(1, -1),
            )
        ]
    )
    new_estimate, resid, owned = pl.pallas_call(
        store_kernel,
        in_specs=[near] * 3,
        out_specs=[kept] * 3,
        out_shape=[pltpu.HBM(*result) for result in results],
        scratch_shapes=[dma((3,))],
    )(*[pltpu.with_memory_space_constraint(result, pltpu.VMEM) for result in made])
    return (new_estimate, resid, owned.reshape(-1))


def solution(mesh):
    device = ("region", "cluster")
    placed = (
        P(device, None, None),
        P(device, None, None),
        P(device, None),
        P(device),
        P(device, None, None),
        P(device, None, None),
        P(device),
        P(),
        P(),
    )
    return jax.shard_map(
        local,
        mesh=mesh,
        in_specs=placed,
        out_specs=(P(device, None, None), P(device, None, None), P(device)),
        check_vma=False,
    )
```
